512 devices in a mesh: rows: 128 (over z, y, core), blk: 4 (over x).
Axes of the slice: x: 4, y: 8, z: 8, core: 2. Of those that a mesh axis runs over, the one named last changes fastest.
Arguments:
- vectors: bfloat16 [64, 131072], P('blk', 'rows'), may hold values from -40 to 40
- hamiltonian: bfloat16 [2048, 64, 8704], P('rows', None, 'blk'), may hold values from -0.078125 to 0.078125
- column_index: int32 [2048, 136], P('rows', 'blk'), may hold values from 0 to 2047, as said below
- counts: int32 [2048], P('rows'), may hold values from 1 to 129, as said below
Outputs:
- basis: float32 [64, 131072], P('blk', 'rows')
- factor: float32 [64, 64], replicated
The draws below stay inside these ranges and needn't reach their ends.
Inputs may be any that keep to these rules, and one draw needn't show every extreme that they name: `column_index`: entry I, s for s < counts[I] is (I + d) mod 2048 for offsets -64 <= d <= 64 that are distinct within a row and listed in rising order; slots past the count hold I. Every row counts its own block; some row uses all 129 offsets.
All inputs are finite; a program needn't handle non-finite values.
Results may differ from the reference program's by a relative error of at most 0.018.
Values may be sent and summed in bfloat16 or wider, within the bound.
No kernel may reach another device: no remote copies, remote signals or barrier semaphores. Data moves between devices by JAX's collectives and lax.ppermute only.
A program may use at most 64 MiB of HBM per device.

```python
import math
import jax
import jax.numpy as jnp
from jax import lax

BS = 64
VECS = 64
HW = 64
NBR = 16
SLOTS = 136
NB = 2048
ORDER = 131072
N_ROWS = 128


LOG_TEN = math.log(10.0)


def coupling_pattern(key):
    sub_key = jax.random.fold_in(key, 7)
    scores = jax.random.randint(sub_key, (NB, 2 * HW + 1), 0, 100)
    offsets = jnp.arange(-HW, HW + 1).astype(jnp.int32)
    row_ids = jnp.arange(NB).astype(jnp.int32)[:, None]
    present = (scores < 78) | (offsets[None, :] == 0) | (row_ids == 0)
    ranking = jnp.argsort(1 - present.astype(jnp.int32), axis=1, stable=True)
    chosen = jnp.take_along_axis(jnp.broadcast_to(offsets[None, :], (NB, 2 * HW + 1)), ranking, axis=1)
    counted = jnp.sum(present.astype(jnp.int32), axis=1).astype(jnp.int32)
    slot_ids = jnp.arange(2 * HW + 1).astype(jnp.int32)[None, :]
    columns = jnp.where(slot_ids < counted[:, None], (row_ids + chosen) % NB, row_ids)
    padding = jnp.broadcast_to(row_ids, (NB, SLOTS - 2 * HW - 1))
    return (jnp.concatenate([columns, padding], axis=1).astype(jnp.int32), counted)


def draw_column_index(key, part):
    return coupling_pattern(key)[0]


def draw_counts(key, part):
    return coupling_pattern(key)[1]


def draw_vectors(key, part):
    key_base = jax.random.fold_in(key, 11)
    key_rows = jax.random.fold_in(key, 12)
    key_cols = jax.random.fold_in(key, 13)
    entries = jnp.clip(jax.random.normal(key_base, (VECS, ORDER), jnp.float32), -4.0, 4.0)
    row_scale = jnp.exp(jax.random.uniform(key_rows, (1, ORDER), jnp.float32) * LOG_TEN)
    col_scale = jnp.exp(jax.random.uniform(key_cols, (VECS, 1), jnp.float32) * LOG_TEN)
    return (0.1 * entries * row_scale * col_scale).astype(jnp.bfloat16)


def block_scale(rng, shape, shards, smallest, high):
    loudness, own = 1.0, jax.random.fold_in(rng, 6)
    for position, blocks in shards:
        steps = jnp.exp(jax.random.uniform(jax.random.fold_in(own, position), (blocks,), jnp.float32, smallest / len(shards), high / len(shards)))
        loudness = loudness * jnp.repeat(steps, shape[position] // blocks).reshape([-1 if axis == position else 1 for axis in range(len(shape))])
    return loudness


def noise(key, shape, scale, bound, shards=(), kind=jnp.bfloat16):
    values = scale * jax.random.normal(key, shape, jnp.float32)
    if shards:
        values = values * block_scale(key, shape, shards, -0.22, 0.18)
    return jnp.clip(values, -bound, bound).astype(kind)


def setup_inputs(seed: int = 0) -> dict:
    arg_keys = jax.random.split(jax.random.key(seed), 5)
    vectors = draw_vectors(jax.random.fold_in(arg_keys[4], 71), 0)
    hamiltonian = noise(arg_keys[1], (NB, BS, SLOTS * BS), (BS * (2 * HW + 1) * 4 // 5) ** -0.5, 0.078125, ((0, 128), (2, 4)))
    column_index = draw_column_index(jax.random.fold_in(arg_keys[4], 71), 0)
    counts = draw_counts(jax.random.fold_in(arg_keys[4], 71), 0)
    return {"vectors": vectors, "hamiltonian": hamiltonian, "column_index": column_index, "counts": counts}


def apply_operator(vectors_in, hamiltonian, column_index, counts):
    vec_blocks = vectors_in.astype(jnp.float32).reshape(VECS, NB, BS)
    ham_groups = hamiltonian.reshape(N_ROWS, NBR, BS, SLOTS, BS)
    col_groups = column_index.reshape(N_ROWS, NBR, SLOTS)
    cnt_groups = counts.reshape(N_ROWS, NBR)
    slot_ids = jnp.arange(SLOTS).astype(jnp.int32)

    def per_group(items):
        ham_group, col_group, cnt_group = items
        picked = vec_blocks[:, col_group, :]
        live_slot = slot_ids[None, :] < cnt_group[:, None]
        picked = jnp.where(live_slot[None, :, :, None], picked, jnp.float32(0.0))
        return jnp.einsum('vrsk,risk->vri', picked, ham_group.astype(jnp.float32), precision=lax.Precision.HIGHEST)
    result = lax.map(per_group, (ham_groups, col_groups, cnt_groups))
    return jnp.transpose(result, (1, 0, 2, 3)).reshape(VECS, ORDER)

def reference(vectors, hamiltonian, column_index, counts):
    first = apply_operator(vectors, hamiltonian, column_index, counts).astype(jnp.bfloat16)
    second = apply_operator(first, hamiltonian, column_index, counts)
    filtered = (2.0 * second - vectors.astype(jnp.float32)).astype(jnp.bfloat16)
    gram = jnp.dot(filtered.astype(jnp.float32), filtered.T.astype(jnp.float32), preferred_element_type=jnp.float32) / ORDER
    lower = jnp.linalg.cholesky(gram)
    basis = lax.linalg.triangular_solve(lower, filtered.astype(jnp.float32), left_side=True, lower=True)
    return (basis, lower.T)
```

```python
import functools

import jax
import jax.numpy as jnp
from jax import lax
from jax.experimental import pallas as pl
from jax.experimental.pallas import tpu as pltpu
from jax.sharding import Mesh, PartitionSpec as P

HW = 64
ROWS = ("z", "y", "core")
F32 = jnp.float32
BF16 = jnp.bfloat16
VMEM_SPEC = pl.BlockSpec(memory_space=pltpu.VMEM)
SMEM_SPEC = pl.BlockSpec(memory_space=pltpu.SMEM)


def call(kernel, out_shape, in_specs, scratch=()):
    outs = jax.tree.map(lambda _: VMEM_SPEC, out_shape)
    return pl.pallas_call(
        kernel, out_shape=out_shape, in_specs=in_specs, out_specs=outs, scratch_shapes=scratch
    )


def shape(dims, dtype):
    return jax.ShapeDtypeStruct(dims, dtype)


def product_kernel(copies, index, *refs):
    pieces, (ham, out, tiles) = refs[:5], refs[5:]
    vecs = ham.shape[1]
    half = lax.broadcasted_iota(jnp.int32, (vecs, 128), 1) < 64
    for p, piece in enumerate(pieces):
        for u in range(2):
            base = 32 * p + 16 * u
            loaded = [piece[u, :, 128 * t : 128 * (t + 1)] for t in range(8)]
            for t in range(8):
                tiles[base + 2 * t] = loaded[t]
                tiles[base + 2 * t + 1] = jnp.concatenate(
                    [loaded[t][:, 64:], loaded[(t + 1) % 8][:, :64]], axis=1
                )
    tiles[160] = jnp.zeros((vecs, 128), BF16)
    pairs = ham.shape[2] // 128

    def two_rows(m, carry):
        sums = []
        for k in range(2):
            row = 2 * m + k
            picked = jnp.concatenate(
                [
                    jnp.where(half, tiles[index[row, 2 * s]], tiles[index[row, 2 * s + 1]])
                    for s in range(pairs)
                ],
                axis=1,
            )
            sums.append(
                lax.dot_general(
                    picked, ham[row], (((1,), (1,)), ((), ())), preferred_element_type=F32
                )
            )
        both = jnp.concatenate(sums, axis=1).astype(BF16)
        lanes = pl.ds(pl.multiple_of(m * 128, 128), 128)
        for c in range(copies):
            out[c, :, lanes] = both
        return carry

    lax.fori_loop(0, ham.shape[0] // 2, two_rows, 0)


def gram_kernel(core, parts, own, filtered, gram):
    total = parts[0].astype(F32)
    for b in range(1, 4):
        total += parts[b].astype(F32)
    value = (2.0 * total - own[core[0]].astype(F32)).astype(BF16)
    filtered[...] = value
    g = lax.dot_general(value, value, (((1,), (1,)), ((), ())), preferred_element_type=F32)
    packed = jnp.concatenate([g[:32], g[32:]], axis=1)
    for c in range(8):
        gram[c] = packed


def sum_kernel(parts, out):
    total = parts[0]
    for c in range(1, 8):
        total += parts[c]
    for c in range(out.shape[0]):
        out[c] = total


def factor_kernel(scale, blk, one, two, filtered, basis, factor, scratch):
    packed = (one[0] + two[0]) * scale
    lane = lax.broadcasted_iota(jnp.int32, (8, 128), 1)
    sub = lax.broadcasted_iota(jnp.int32, (8, 128), 0)
    chunks = []
    for c in range(8):
        rows = packed[8 * (c % 4) : 8 * (c % 4) + 8]
        if c >= 4:
            rows = jnp.concatenate([rows[:, 64:], rows[:, :64]], axis=1)
        eye = jnp.where(lane - 64 == sub + 8 * c, F32(1.0), F32(0.0))
        chunks.append(jnp.where(lane < 64, rows, eye))
    for k in range(64):
        ck, r = divmod(k, 8)
        row = chunks[ck][r : r + 1]
        inv = 1.0 / jnp.sqrt(row[:, k : k + 1])
        unit = row * inv
        for c in range(ck, 8):
            col = chunks[c][:, k : k + 1] * inv
            if c == ck:
                moved = jnp.where(sub > r, chunks[c] - col * unit, chunks[c])
                chunks[c] = jnp.where(sub == r, jnp.broadcast_to(unit, (8, 128)), moved)
            else:
                chunks[c] = chunks[c] - col * unit
    for c in range(8):
        keep = jnp.where(lane >= sub + 8 * c, chunks[c], F32(0.0))
        factor[8 * c : 8 * c + 8, :] = keep[:, :64]
        scratch[8 * c : 8 * c + 8, :] = chunks[c][:, 64:]
    mine = scratch[pl.ds(pl.multiple_of(blk[0] * 16, 16), 16), :]
    total = jnp.zeros(basis.shape, F32)
    rest = mine
    parts = []
    for _ in range(3):
        top = rest.astype(BF16)
        parts.append(top)
        rest = rest - top.astype(F32)
    for top in reversed(parts):
        total += jnp.dot(top, filtered[...], preferred_element_type=F32)
    basis[...] = total


def from_chip(value, distance):
    chips = lax.axis_size("z") * lax.axis_size("y")
    pairs = []
    for c in range(chips):
        pairs.append((2 * ((c - distance) % chips), 2 * c))
        pairs.append((2 * ((c + distance) % chips) + 1, 2 * c + 1))
    return lax.ppermute(value, ROWS, pairs)


def flip(value):
    return lax.ppermute(value, "core", [(0, 1), (1, 0)])


def window(pair):
    far = from_chip(pair, 2)
    near = from_chip(pair, 1)
    far_other = flip(far)
    near_other = flip(near)
    return far, near, pair, near_other, far_other


def to_all(value, axes, count):
    return lax.all_to_all(
        jnp.broadcast_to(value[None], (count,) + value.shape), axes, 0, 0, tiled=True
    )


def body(vectors, hamiltonian, column_index, counts):
    block_rows = counts.shape[0]
    width = hamiltonian.shape[1]
    slots_here = column_index.shape[1]
    vecs = width
    core = lax.axis_index("core")
    blk = lax.axis_index("blk")
    chip = lax.axis_index("z") * lax.axis_size("y") + lax.axis_index("y")
    total_blocks = block_rows * lax.axis_size(ROWS)

    offset = (column_index - (chip - 2) * 2 * block_rows) % total_blocks
    slot_ids = lax.broadcasted_iota(jnp.int32, column_index.shape, 1)
    live = slot_ids + blk * slots_here < counts[:, None]
    away, within = offset // 32, offset % 32
    place = jnp.where(core == 0, away, 4 - away) * 32 + (within // 16) * 16
    block = within % 16
    tile = place + jnp.where(slot_ids % 2 == 0, block, (block + 15) % 16)
    index = jnp.where(live, tile, 160)

    core_id = core.reshape(1).astype(jnp.int32)
    blk_id = blk.reshape(1).astype(jnp.int32)

    def products(pieces, copies):
        return call(
            functools.partial(product_kernel, copies),
            shape((copies, vecs, block_rows * width), BF16),
            [SMEM_SPEC] + [VMEM_SPEC] * 6,
            [pltpu.VMEM((161, vecs, 128), BF16)],
        )(index, *pieces, hamiltonian)

    pair = to_all(vectors, ("core", "blk"), 8).reshape(2, vecs, block_rows * width)
    parts = products(window(pair), 4)
    parts = lax.all_to_all(parts, "blk", 0, 0, tiled=True)
    first = jnp.sum(parts.astype(F32), axis=0).astype(BF16)
    other = flip(first)
    pair_two = jnp.where(core == 0, jnp.stack([first, other]), jnp.stack([other, first]))
    parts = products(window(pair_two), 4)
    parts = lax.all_to_all(parts, "blk", 0, 0, tiled=True)
    filtered, gram = call(
        gram_kernel,
        (shape((vecs, block_rows * width), BF16), shape((8, 32, 128), F32)),
        [SMEM_SPEC, VMEM_SPEC, VMEM_SPEC],
    )(core_id, parts, pair)
    gram = lax.all_to_all(gram, "y", 0, 0, tiled=True)
    gram = call(sum_kernel, shape((8, 32, 128), F32), [VMEM_SPEC])(gram)
    gram = lax.all_to_all(gram, "z", 0, 0, tiled=True)
    gram = call(sum_kernel, shape((1, 32, 128), F32), [VMEM_SPEC])(gram)
    basis, factor = call(
        functools.partial(factor_kernel, 1.0 / (total_blocks * width)),
        (shape(vectors.shape, F32), shape((vecs, vecs), F32)),
        [SMEM_SPEC] + [VMEM_SPEC] * 3,
        [pltpu.VMEM((vecs, vecs), F32)],
    )(blk_id, gram, flip(gram), filtered)
    return basis, factor


def solution(mesh):
    chips = mesh.shape["rows"] // 2
    y = 8
    fine = Mesh(
        mesh.devices.reshape(chips // y, y, 2, mesh.shape["blk"]), ("z", "y", "core", "blk")
    )
    in_specs = (P("blk", ROWS), P(ROWS, None, "blk"), P(ROWS, "blk"), P(ROWS))
    out_specs = (P("blk", ROWS), P())
    return jax.shard_map(body, mesh=fine, in_specs=in_specs, out_specs=out_specs, check_vma=False)
```

```python
import functools

import jax
import jax.numpy as jnp
from jax import lax
from jax.experimental import pallas as pl
from jax.experimental.pallas import tpu as pltpu
from jax.sharding import Mesh, PartitionSpec as P

HW = 64
ROWS = ("z", "y", "core")
F32 = jnp.float32
BF16 = jnp.bfloat16
VMEM_SPEC = pl.BlockSpec(memory_space=pltpu.VMEM)
SMEM_SPEC = pl.BlockSpec(memory_space=pltpu.SMEM)


def call(kernel, out_shape, in_specs, scratch=(), mib=4):
    outs = jax.tree.map(lambda _: VMEM_SPEC, out_shape)
    return pl.pallas_call(
        kernel,
        out_shape=out_shape,
        in_specs=in_specs,
        out_specs=outs,
        scratch_shapes=scratch,
        compiler_params=pltpu.CompilerParams(vmem_limit_bytes=mib << 20),
    )


def shape(dims, dtype):
    return jax.ShapeDtypeStruct(dims, dtype)


def product_kernel(copies, index, *refs):
    pieces, (ham, out, tiles) = refs[:5], refs[5:]
    vecs = ham.shape[1]
    half = lax.broadcasted_iota(jnp.int32, (vecs, 128), 1) < 64
    for p, piece in enumerate(pieces):
        for u in range(2):
            base = 32 * p + 16 * u
            loaded = [piece[u, :, 128 * t : 128 * (t + 1)] for t in range(8)]
            for t in range(8):
                tiles[base + 2 * t] = loaded[t]
                tiles[base + 2 * t + 1] = jnp.concatenate(
                    [loaded[t][:, 64:], loaded[(t + 1) % 8][:, :64]], axis=1
                )
    tiles[160] = jnp.zeros((vecs, 128), BF16)
    pairs = ham.shape[2] // 128

    def two_rows(m, carry):
        sums = []
        for k in range(2):
            row = 2 * m + k
            picked = jnp.concatenate(
                [
                    jnp.where(half, tiles[index[row, 2 * s]], tiles[index[row, 2 * s + 1]])
                    for s in range(pairs)
                ],
                axis=1,
            )
            sums.append(
                lax.dot_general(
                    picked, ham[row], (((1,), (1,)), ((), ())), preferred_element_type=F32
                )
            )
        both = jnp.concatenate(sums, axis=1).astype(BF16)
        lanes = pl.ds(pl.multiple_of(m * 128, 128), 128)
        for c in range(copies):
            out[c, :, lanes] = both
        return carry

    lax.fori_loop(0, ham.shape[0] // 2, two_rows, 0)


def gram_kernel(core, parts, own, filtered, gram):
    total = parts[0].astype(F32)
    for b in range(1, 4):
        total += parts[b].astype(F32)
    value = (2.0 * total - own[core[0]].astype(F32)).astype(BF16)
    filtered[...] = value
    g = lax.dot_general(value, value, (((1,), (1,)), ((), ())), preferred_element_type=F32)
    packed = jnp.concatenate([g[:32], g[32:]], axis=1)
    for c in range(gram.shape[0]):
        gram[c] = packed


def sum_kernel(parts, out):
    total = parts[0]
    for c in range(1, parts.shape[0]):
        total += parts[c]
    for c in range(out.shape[0]):
        out[c] = total


def factor_kernel(scale, blk, parts, filtered, basis, factor, scratch):
    total = parts[0]
    for c in range(1, 8):
        total += parts[c]
    packed = total * scale
    lane = lax.broadcasted_iota(jnp.int32, (8, 128), 1)
    sub = lax.broadcasted_iota(jnp.int32, (8, 128), 0)
    chunks = []
    for c in range(8):
        rows = packed[8 * (c % 4) : 8 * (c % 4) + 8]
        if c >= 4:
            rows = jnp.concatenate([rows[:, 64:], rows[:, :64]], axis=1)
        eye = jnp.where(lane - 64 == sub + 8 * c, F32(1.0), F32(0.0))
        chunks.append(jnp.where(lane < 64, rows, eye))
    for k in range(63):
        ck, r = divmod(k, 8)
        row = jnp.broadcast_to(chunks[ck][r : r + 1], (8, 128))
        lead = jnp.broadcast_to(chunks[ck][:, k : k + 1], (8, 128))
        inv = 1.0 / jnp.broadcast_to(lead[r : r + 1], (8, 128))
        if r < 7:
            times = jnp.where(sub > r, lead * inv, F32(0.0))
            chunks[ck] = chunks[ck] - times * row
        for c in range(ck + 1, 8):
            lead = jnp.broadcast_to(chunks[c][:, k : k + 1], (8, 128))
            chunks[c] = chunks[c] - (lead * inv) * row
    for c in range(8):
        pivot = jnp.where(lane == sub + 8 * c, chunks[c], F32(0.0))
        root = 1.0 / jnp.sqrt(jnp.sum(pivot, axis=1, keepdims=True))
        scaled = chunks[c] * root
        keep = jnp.where(lane >= sub + 8 * c, scaled, F32(0.0))
        factor[8 * c : 8 * c + 8, :] = keep[:, :64]
        scratch[8 * c : 8 * c + 8, :] = scaled[:, 64:]
    mine = scratch[pl.ds(pl.multiple_of(blk[0] * 16, 16), 16), :]
    total = jnp.zeros(basis.shape, F32)
    rest = mine
    parts = []
    for _ in range(3):
        top = rest.astype(BF16)
        parts.append(top)
        rest = rest - top.astype(F32)
    for top in reversed(parts):
        total += jnp.dot(top, filtered[...], preferred_element_type=F32)
    basis[...] = total


def from_chip(value, distance):
    chips = lax.axis_size("z") * lax.axis_size("y")
    pairs = []
    for c in range(chips):
        pairs.append((2 * ((c - distance) % chips), 2 * c))
        pairs.append((2 * ((c + distance) % chips) + 1, 2 * c + 1))
    return lax.ppermute(value, ROWS, pairs)


def flip(value):
    return lax.ppermute(value, "core", [(0, 1), (1, 0)])


def window(pair):
    far = from_chip(pair, 2)
    near = from_chip(pair, 1)
    far_other = flip(far)
    near_other = flip(near)
    return far, near, pair, near_other, far_other


def to_all(value, axes, count):
    return lax.all_to_all(
        jnp.broadcast_to(value[None], (count,) + value.shape), axes, 0, 0, tiled=True
    )


def body(vectors, hamiltonian, column_index, counts):
    block_rows = counts.shape[0]
    width = hamiltonian.shape[1]
    slots_here = column_index.shape[1]
    vecs = width
    core = lax.axis_index("core")
    blk = lax.axis_index("blk")
    chip = lax.axis_index("z") * lax.axis_size("y") + lax.axis_index("y")
    total_blocks = block_rows * lax.axis_size(ROWS)

    offset = (column_index - (chip - 2) * 2 * block_rows) % total_blocks
    slot_ids = lax.broadcasted_iota(jnp.int32, column_index.shape, 1)
    live = slot_ids + blk * slots_here < counts[:, None]
    away, within = offset // 32, offset % 32
    place = jnp.where(core == 0, away, 4 - away) * 32 + (within // 16) * 16
    block = within % 16
    tile = place + jnp.where(slot_ids % 2 == 0, block, (block + 15) % 16)
    index = jnp.where(live, tile, 160)

    core_id = core.reshape(1).astype(jnp.int32)
    blk_id = blk.reshape(1).astype(jnp.int32)

    def products(pieces, copies):
        return call(
            functools.partial(product_kernel, copies),
            shape((copies, vecs, block_rows * width), BF16),
            [SMEM_SPEC] + [VMEM_SPEC] * 6,
            [pltpu.VMEM((161, vecs, 128), BF16)],
            12,
        )(index, *pieces, hamiltonian)

    pair = to_all(vectors, ("core", "blk"), 8).reshape(2, vecs, block_rows * width)
    parts = products(window(pair), 4)
    parts = lax.all_to_all(parts, "blk", 0, 0, tiled=True)
    first = jnp.sum(parts.astype(F32), axis=0).astype(BF16)
    other = flip(first)
    pair_two = jnp.where(core == 0, jnp.stack([first, other]), jnp.stack([other, first]))
    parts = products(window(pair_two), 4)
    parts = lax.all_to_all(parts, "blk", 0, 0, tiled=True)
    filtered, gram = call(
        gram_kernel,
        (shape((vecs, block_rows * width), BF16), shape((16, 32, 128), F32)),
        [SMEM_SPEC, VMEM_SPEC, VMEM_SPEC],
    )(core_id, parts, pair)
    gram = lax.all_to_all(gram, ("y", "core"), 0, 0, tiled=True)
    gram = call(sum_kernel, shape((8, 32, 128), F32), [VMEM_SPEC])(gram)
    gram = lax.all_to_all(gram, "z", 0, 0, tiled=True)
    basis, factor = call(
        functools.partial(factor_kernel, 1.0 / (total_blocks * width)),
        (shape(vectors.shape, F32), shape((vecs, vecs), F32)),
        [SMEM_SPEC] + [VMEM_SPEC] * 2,
        [pltpu.VMEM((vecs, vecs), F32)],
    )(blk_id, gram, filtered)
    return basis, factor


def solution(mesh):
    chips = mesh.shape["rows"] // 2
    y = 8
    fine = Mesh(
        mesh.devices.reshape(chips // y, y, 2, mesh.shape["blk"]), ("z", "y", "core", "blk")
    )
    in_specs = (P("blk", ROWS), P(ROWS, None, "blk"), P(ROWS, "blk"), P(ROWS))
    out_specs = (P("blk", ROWS), P())
    return jax.shard_map(body, mesh=fine, in_specs=in_specs, out_specs=out_specs, check_vma=False)
```

```python
import functools

import jax
import jax.numpy as jnp
from jax import lax
from jax.experimental import pallas as pl
from jax.experimental.pallas import tpu as pltpu
from jax.sharding import Mesh, PartitionSpec as P

HW = 64
ROWS = ("z", "y", "core")
F32 = jnp.float32
BF16 = jnp.bfloat16
VMEM_SPEC = pl.BlockSpec(memory_space=pltpu.VMEM)
ANY_SPEC = pl.BlockSpec(memory_space=pl.ANY)
SMEM_SPEC = pl.BlockSpec(memory_space=pltpu.SMEM)


def call(kernel, out_shape, in_specs, scratch=(), mib=4):
    outs = jax.tree.map(lambda _: VMEM_SPEC, out_shape)
    return pl.pallas_call(
        kernel,
        out_shape=out_shape,
        in_specs=in_specs,
        out_specs=outs,
        scratch_shapes=scratch,
        compiler_params=pltpu.CompilerParams(vmem_limit_bytes=mib << 20),
    )


def shape(dims, dtype):
    return jax.ShapeDtypeStruct(dims, dtype)


def product_kernel(copies, index, *refs):
    pieces, (ham, out, tiles) = refs[:5], refs[5:]
    vecs = ham.shape[1]
    half = lax.broadcasted_iota(jnp.int16, (vecs, 128), 1) < jnp.int16(64)
    for p, piece in enumerate(pieces):
        for u in range(2):
            base = 32 * p + 16 * u
            start = here = piece[u, :, :128]
            for t in range(8):
                after = start if t == 7 else piece[u, :, 128 * (t + 1) : 128 * (t + 2)]
                tiles[base + 2 * t] = here
                tiles[base + 2 * t + 1] = pltpu.roll(jnp.where(half, after, here), 64, 1)
                here = after
    tiles[160] = jnp.zeros((vecs, 128), BF16)
    pairs = ham.shape[2] // 128

    def picked(row):
        return jnp.concatenate(
            [
                jnp.where(half, tiles[index[row, 2 * s]], tiles[index[row, 2 * s + 1]])
                for s in range(pairs)
            ],
            axis=1,
        )

    def two_rows(m, carry):
        sums = []
        for k in range(2):
            row = 2 * m + k
            sums.append(
                lax.dot_general(
                    picked(row), ham[row], (((1,), (1,)), ((), ())), preferred_element_type=F32
                )
            )
        both = jnp.concatenate(sums, axis=1).astype(BF16)
        lanes = pl.ds(pl.multiple_of(m * 128, 128), 128)
        for c in range(copies):
            out[c, :, lanes] = both
        return carry

    lax.fori_loop(0, ham.shape[0] // 2, two_rows, 0, unroll=4)


def index_kernel(total_blocks, block_rows, columns, counts, ham, out):
    core, blk = lax.axis_index("core"), lax.axis_index("blk")
    chip = lax.axis_index("z") * lax.axis_size("y") + lax.axis_index("y")
    slot = lax.broadcasted_iota(jnp.int32, columns.shape, 1)
    live = slot + blk * columns.shape[1] < counts[...]
    offset = (columns[...] - (chip - 2) * 2 * block_rows) & (total_blocks - 1)
    away, block = offset >> 5, offset & 15
    place = jnp.where(core == 0, away, 4 - away) * 32 + (offset & 16)
    tile = place + jnp.where((slot & 1) == 0, block, (block + 15) & 15)
    out[...] = jnp.where(live, tile, 160)


def first_kernel(parts, out):
    total = parts[0].astype(F32)
    for b in range(1, 4):
        total += parts[b].astype(F32)
    out[...] = total.astype(BF16)


def pair_kernel(mine, other, out):
    core = lax.axis_index("core")
    out[core] = mine[...]
    out[1 - core] = other[...]


STRIPS = ((7, 6, 0), (5, 4, 3), (2, 1))


def pack(g):
    lane = lax.broadcasted_iota(jnp.int32, (8, 128), 1)
    rows = []
    for group in STRIPS:
        at, line = 0, jnp.zeros((8, 128), F32)
        for i in group:
            wide = jnp.concatenate([g[8 * i : 8 * i + 8], jnp.zeros((8, 64), F32)], axis=1)
            moved = pltpu.roll(wide, at, 1) if at else wide
            line = jnp.where((lane >= at) & (lane < at + 8 * i + 8), moved, line)
            at += 8 * i + 8
        rows.append(line)
    return jnp.concatenate(rows, axis=0)


def unpack(packed):
    strips = [None] * 8
    for q, group in enumerate(STRIPS):
        at, line = 0, packed[8 * q : 8 * q + 8]
        for i in group:
            strips[i] = (pltpu.roll(line, 128 - at, 1) if at else line)[:, :64]
            at += 8 * i + 8
    low = jnp.concatenate(strips, axis=0)
    row = lax.broadcasted_iota(jnp.int32, (64, 64), 0) // 8
    col = lax.broadcasted_iota(jnp.int32, (64, 64), 1) // 8
    return jnp.where(col <= row, low, low.T)


def gram_kernel(parts, own, filtered, gram):
    total = parts[0].astype(F32)
    for b in range(1, 4):
        total += parts[b].astype(F32)
    value = (2.0 * total - own[lax.axis_index("core")].astype(F32)).astype(BF16)
    filtered[...] = value
    g = lax.dot_general(value, value, (((1,), (1,)), ((), ())), preferred_element_type=F32)
    packed = pack(g)
    for c in range(gram.shape[0]):
        gram[c] = packed


def sum_kernel(parts, out):
    total = parts[0]
    for c in range(1, parts.shape[0]):
        total += parts[c]
    for c in range(out.shape[0]):
        out[c] = total


def factor_kernel(scale, parts, filtered, basis, factor, scratch):
    total = parts[0]
    for c in range(1, 8):
        total += parts[c]
    whole = unpack(total * scale)
    lane = lax.broadcasted_iota(jnp.int32, (8, 128), 1)
    sub = lax.broadcasted_iota(jnp.int32, (8, 128), 0)
    zero = jnp.zeros((8, 64), F32)
    chunks = []
    for c in range(8):
        eye = jnp.where(lane - 64 == sub + 8 * c, F32(1.0), F32(0.0))
        wide = jnp.concatenate([whole[8 * c : 8 * c + 8], zero], axis=1)
        chunks.append(jnp.where(lane < 64, wide, eye))

    def spread(chunk, k):
        value = jnp.sum(jnp.where(lane == k, chunk, F32(0.0)), axis=1, keepdims=True)
        return jnp.broadcast_to(value, (8, 128))

    def down(value, r):
        return jnp.broadcast_to(value[r : r + 1], (8, 128))

    for b in range(8):
        cols = {c: [spread(chunks[c], 8 * b + j) for j in range(8)] for c in range(b, 8)}
        for r in range(8):
            row = down(chunks[b], r)
            heads = [down(cols[b][j], r) for j in range(r, 8)]
            inv = 1.0 / heads[0]
            for c in range(b if r < 7 else b + 1, 8):
                times = cols[c][r] * inv
                if c == b:
                    times = jnp.where(sub > r, times, F32(0.0))
                chunks[c] = chunks[c] - times * row
                for j in range(r + 1, 8):
                    cols[c][j] = cols[c][j] - times * heads[j - r]
    for c in range(8):
        pivot = jnp.where(lane == sub + 8 * c, chunks[c], F32(0.0))
        root = 1.0 / jnp.sqrt(jnp.sum(pivot, axis=1, keepdims=True))
        scaled = chunks[c] * root
        keep = jnp.where(lane >= sub + 8 * c, scaled, F32(0.0))
        factor[8 * c : 8 * c + 8, :] = keep[:, :64]
        scratch[8 * c : 8 * c + 8, :] = scaled[:, 64:]
    mine = scratch[pl.ds(pl.multiple_of(lax.axis_index("blk") * 16, 16), 16), :]
    total = jnp.zeros(basis.shape, F32)
    rest = mine
    parts = []
    for _ in range(3):
        top = rest.astype(BF16)
        parts.append(top)
        rest = rest - top.astype(F32)
    for top in reversed(parts):
        total += jnp.dot(top, filtered[...], preferred_element_type=F32)
    basis[...] = total


def from_chip(value, distance):
    chips = lax.axis_size("z") * lax.axis_size("y")
    pairs = []
    for c in range(chips):
        pairs.append((2 * ((c - distance) % chips), 2 * c))
        pairs.append((2 * ((c + distance) % chips) + 1, 2 * c + 1))
    return lax.ppermute(value, ROWS, pairs)


def flip(value):
    return lax.ppermute(value, "core", [(0, 1), (1, 0)])


def window(pair, beside=None):
    near = from_chip(pair, 1)
    far = from_chip(pair, 2)
    if beside is not None:
        near, beside = lax.optimization_barrier((near, beside))
    far_other = flip(far)
    near_other = flip(near)
    return (far, near, pair, near_other, far_other), beside


def to_all(value, axes, count):
    return lax.all_to_all(
        jnp.broadcast_to(value[None], (count,) + value.shape), axes, 0, 0, tiled=True
    )


def body(vectors, hamiltonian, column_index, counts):
    block_rows = counts.shape[0]
    width = hamiltonian.shape[1]
    vecs = width
    total_blocks = block_rows * lax.axis_size(ROWS)
    index = call(
        functools.partial(index_kernel, total_blocks, block_rows),
        shape(column_index.shape, jnp.int32),
        [VMEM_SPEC] * 2 + [ANY_SPEC],
    )(column_index, counts.reshape(block_rows, 1), hamiltonian)

    def products(pieces, index, copies):
        return call(
            functools.partial(product_kernel, copies),
            shape((copies, vecs, block_rows * width), BF16),
            [SMEM_SPEC] + [VMEM_SPEC] * 6,
            [pltpu.VMEM((161, vecs, 128), BF16)],
            12,
        )(index, *pieces, hamiltonian)

    pair = to_all(vectors, ("core", "blk"), 8).reshape(2, vecs, block_rows * width)
    pieces, index = window(pair, index)
    parts = products(pieces, index, 4)
    parts = lax.all_to_all(parts, "blk", 0, 0, tiled=True)
    unit = shape((vecs, block_rows * width), BF16)
    first = call(first_kernel, unit, [VMEM_SPEC])(parts)
    pair_two = call(pair_kernel, shape(pair.shape, BF16), [VMEM_SPEC] * 2)(first, flip(first))
    parts = products(window(pair_two)[0], index, 4)
    parts = lax.all_to_all(parts, "blk", 0, 0, tiled=True)
    filtered, gram = call(
        gram_kernel,
        (unit, shape((16, 24, 128), F32)),
        [VMEM_SPEC] * 2,
    )(parts, pair)
    gram = lax.all_to_all(gram, ("y", "core"), 0, 0, tiled=True)
    gram = call(sum_kernel, shape((8, 24, 128), F32), [VMEM_SPEC])(gram)
    gram = lax.all_to_all(gram, "z", 0, 0, tiled=True)
    basis, factor = call(
        functools.partial(factor_kernel, 1.0 / (total_blocks * width)),
        (shape(vectors.shape, F32), shape((vecs, vecs), F32)),
        [VMEM_SPEC] * 2,
        [pltpu.VMEM((vecs, vecs), F32)],
    )(gram, filtered)
    return basis, factor


def solution(mesh):
    chips = mesh.shape["rows"] // 2
    y = 8
    fine = Mesh(
        mesh.devices.reshape(chips // y, y, 2, mesh.shape["blk"]), ("z", "y", "core", "blk")
    )
    in_specs = (P("blk", ROWS), P(ROWS, None, "blk"), P(ROWS, "blk"), P(ROWS))
    out_specs = (P("blk", ROWS), P())
    return jax.shard_map(body, mesh=fine, in_specs=in_specs, out_specs=out_specs, check_vma=False)
```

```python
import functools

import jax
import jax.numpy as jnp
from jax import lax
from jax.experimental import pallas as pl
from jax.experimental.pallas import tpu as pltpu
from jax.sharding import Mesh, PartitionSpec as P

ROWS = ("z", "y", "core")
F32 = jnp.float32
BF16 = jnp.bfloat16
VMEM_SPEC = pl.BlockSpec(memory_space=pltpu.VMEM)
ANY_SPEC = pl.BlockSpec(memory_space=pl.ANY)
SMEM_SPEC = pl.BlockSpec(memory_space=pltpu.SMEM)


def call(kernel, out_shape, in_specs, scratch=(), mib=4):
    outs = jax.tree.map(lambda _: VMEM_SPEC, out_shape)
    return pl.pallas_call(
        kernel,
        out_shape=out_shape,
        in_specs=in_specs,
        out_specs=outs,
        scratch_shapes=scratch,
        compiler_params=pltpu.CompilerParams(vmem_limit_bytes=mib << 20),
    )


def shape(dims, dtype):
    return jax.ShapeDtypeStruct(dims, dtype)


def product_kernel(copies, index, *refs):
    pieces, (ham, out, tiles) = refs[:5], refs[5:]
    vecs = ham.shape[1]
    half = lax.broadcasted_iota(jnp.int16, (vecs, 128), 1) < jnp.int16(64)
    for p, piece in enumerate(pieces):
        for u in range(2):
            base = 32 * p + 16 * u
            start = here = piece[u, :, :128]
            for t in range(8):
                after = start if t == 7 else piece[u, :, 128 * (t + 1) : 128 * (t + 2)]
                tiles[base + 2 * t] = here
                tiles[base + 2 * t + 1] = pltpu.roll(jnp.where(half, after, here), 64, 1)
                here = after
    tiles[160] = jnp.zeros((vecs, 128), BF16)
    pairs = ham.shape[2] // 128

    def picked(row):
        return jnp.concatenate(
            [
                jnp.where(half, tiles[index[row, 2 * s]], tiles[index[row, 2 * s + 1]])
                for s in range(pairs)
            ],
            axis=1,
        )

    def two_rows(m, carry):
        sums = []
        for k in range(2):
            row = 2 * m + k
            sums.append(
                lax.dot_general(
                    picked(row), ham[row], (((1,), (1,)), ((), ())), preferred_element_type=F32
                )
            )
        both = jnp.concatenate(sums, axis=1).astype(BF16)
        lanes = pl.ds(pl.multiple_of(m * 128, 128), 128)
        for c in range(copies):
            out[c, :, lanes] = both
        return carry

    lax.fori_loop(0, ham.shape[0] // 2, two_rows, 0, unroll=4)


def index_kernel(total_blocks, block_rows, columns, counts, ham, out):
    core, blk = lax.axis_index("core"), lax.axis_index("blk")
    chip = lax.axis_index("z") * lax.axis_size("y") + lax.axis_index("y")
    slot = lax.broadcasted_iota(jnp.int32, columns.shape, 1)
    live = slot + blk * columns.shape[1] < counts[...]
    offset = (columns[...] - (chip - 2) * 2 * block_rows) & (total_blocks - 1)
    away, block = offset >> 5, offset & 15
    place = jnp.where(core == 0, away, 4 - away) * 32 + (offset & 16)
    tile = place + jnp.where((slot & 1) == 0, block, (block + 15) & 15)
    out[...] = jnp.where(live, tile, 160)


def first_kernel(parts, out):
    total = parts[0].astype(F32)
    for b in range(1, 4):
        total += parts[b].astype(F32)
    out[...] = total.astype(BF16)


def pair_kernel(mine, other, out):
    core = lax.axis_index("core")
    out[core] = mine[...]
    out[1 - core] = other[...]


STRIPS = ((7, 6, 0), (5, 4, 3), (2, 1))


def pack(g):
    lane = lax.broadcasted_iota(jnp.int32, (8, 128), 1)
    rows = []
    for group in STRIPS:
        at, line = 0, jnp.zeros((8, 128), F32)
        for i in group:
            wide = jnp.concatenate([g[8 * i : 8 * i + 8], jnp.zeros((8, 64), F32)], axis=1)
            moved = pltpu.roll(wide, at, 1) if at else wide
            line = jnp.where((lane >= at) & (lane < at + 8 * i + 8), moved, line)
            at += 8 * i + 8
        rows.append(line)
    return jnp.concatenate(rows, axis=0)


def unpack(packed):
    strips = [None] * 8
    for q, group in enumerate(STRIPS):
        at, line = 0, packed[8 * q : 8 * q + 8]
        for i in group:
            strips[i] = (pltpu.roll(line, 128 - at, 1) if at else line)[:, :64]
            at += 8 * i + 8
    low = jnp.concatenate(strips, axis=0)
    row = lax.broadcasted_iota(jnp.int32, (64, 64), 0) // 8
    col = lax.broadcasted_iota(jnp.int32, (64, 64), 1) // 8
    return jnp.where(col <= row, low, low.T)


def gram_kernel(parts, own, filtered, gram):
    total = parts[0].astype(F32)
    for b in range(1, 4):
        total += parts[b].astype(F32)
    value = (2.0 * total - own[lax.axis_index("core")].astype(F32)).astype(BF16)
    filtered[...] = value
    g = lax.dot_general(value, value, (((1,), (1,)), ((), ())), preferred_element_type=F32)
    packed = pack(g)
    for c in range(gram.shape[0]):
        gram[c] = packed


def sum_kernel(parts, out):
    total = parts[0]
    for c in range(1, parts.shape[0]):
        total += parts[c]
    for c in range(out.shape[0]):
        out[c] = total


def factor_kernel(scale, parts, filtered, basis, factor, scratch):
    total = parts[0]
    for c in range(1, 8):
        total += parts[c]
    whole = unpack(total * scale)
    lane = lax.broadcasted_iota(jnp.int32, (8, 128), 1)
    sub = lax.broadcasted_iota(jnp.int32, (8, 128), 0)
    zero = jnp.zeros((8, 64), F32)
    chunks = []
    for c in range(8):
        eye = jnp.where(lane - 64 == sub + 8 * c, F32(1.0), F32(0.0))
        wide = jnp.concatenate([whole[8 * c : 8 * c + 8], zero], axis=1)
        chunks.append(jnp.where(lane < 64, wide, eye))

    def spread(chunk, k):
        value = jnp.sum(jnp.where(lane == k, chunk, F32(0.0)), axis=1, keepdims=True)
        return jnp.broadcast_to(value, (8, 128))

    def down(value, r):
        return jnp.broadcast_to(value[r : r + 1], (8, 128))

    for b in range(8):
        cols = {c: [spread(chunks[c], 8 * b + j) for j in range(8)] for c in range(b, 8)}
        for r in range(8):
            row = down(chunks[b], r)
            heads = [down(cols[b][j], r) for j in range(r, 8)]
            inv = 1.0 / heads[0]
            for c in range(b if r < 7 else b + 1, 8):
                times = cols[c][r] * inv
                if c == b:
                    times = jnp.where(sub > r, times, F32(0.0))
                chunks[c] = chunks[c] - times * row
                for j in range(r + 1, 8):
                    cols[c][j] = cols[c][j] - times * heads[j - r]
    for c in range(8):
        pivot = jnp.where(lane == sub + 8 * c, chunks[c], F32(0.0))
        root = 1.0 / jnp.sqrt(jnp.sum(pivot, axis=1, keepdims=True))
        scaled = chunks[c] * root
        keep = jnp.where(lane >= sub + 8 * c, scaled, F32(0.0))
        factor[8 * c : 8 * c + 8, :] = keep[:, :64]
        scratch[8 * c : 8 * c + 8, :] = scaled[:, 64:]
    mine = scratch[pl.ds(pl.multiple_of(lax.axis_index("blk") * 16, 16), 16), :]
    total = jnp.zeros(basis.shape, F32)
    rest = mine
    parts = []
    for _ in range(3):
        top = rest.astype(BF16)
        parts.append(top)
        rest = rest - top.astype(F32)
    for top in reversed(parts):
        total += jnp.dot(top, filtered[...], preferred_element_type=F32)
    basis[...] = total


def from_chip(value, distance):
    chips = lax.axis_size("z") * lax.axis_size("y")
    pairs = []
    for c in range(chips):
        pairs.append((2 * ((c - distance) % chips), 2 * c))
        pairs.append((2 * ((c + distance) % chips) + 1, 2 * c + 1))
    return lax.ppermute(value, ROWS, pairs)


def flip(value):
    return lax.ppermute(value, "core", [(0, 1), (1, 0)])


def window(pair):
    near = from_chip(pair, 1)
    far = from_chip(pair, -2)
    near_other = flip(near)
    far_other = flip(far)
    return far_other, near, pair, near_other, far


def to_all(value, axes, count):
    return lax.all_to_all(
        jnp.broadcast_to(value[None], (count,) + value.shape), axes, 0, 0, tiled=True
    )


def program(vectors, hamiltonian, column_index, counts):
    block_rows = counts.shape[0]
    width = hamiltonian.shape[1]
    vecs = width
    total_blocks = block_rows * lax.axis_size(ROWS)
    index = call(
        functools.partial(index_kernel, total_blocks, block_rows),
        shape(column_index.shape, jnp.int32),
        [VMEM_SPEC] * 2 + [ANY_SPEC],
    )(column_index, counts.reshape(block_rows, 1), hamiltonian)

    def products(pieces, copies):
        return call(
            functools.partial(product_kernel, copies),
            shape((copies, vecs, block_rows * width), BF16),
            [SMEM_SPEC] + [VMEM_SPEC] * 6,
            [pltpu.VMEM((161, vecs, 128), BF16)],
            12,
        )(index, *pieces, hamiltonian)

    pair = to_all(vectors, ("core", "blk"), 8).reshape(2, vecs, block_rows * width)
    parts = products(window(pair), 4)
    parts = lax.all_to_all(parts, "blk", 0, 0, tiled=True)
    unit = shape((vecs, block_rows * width), BF16)
    first = call(first_kernel, unit, [VMEM_SPEC])(parts)
    pair_two = call(pair_kernel, shape(pair.shape, BF16), [VMEM_SPEC] * 2)(first, flip(first))
    parts = products(window(pair_two), 4)
    parts = lax.all_to_all(parts, "blk", 0, 0, tiled=True)
    filtered, gram = call(
        gram_kernel,
        (unit, shape((16, 24, 128), F32)),
        [VMEM_SPEC] * 2,
    )(parts, pair)
    gram = lax.all_to_all(gram, ("y", "core"), 0, 0, tiled=True)
    gram = call(sum_kernel, shape((8, 24, 128), F32), [VMEM_SPEC])(gram)
    gram = lax.all_to_all(gram, "z", 0, 0, tiled=True)
    basis, factor = call(
        functools.partial(factor_kernel, 1.0 / (total_blocks * width)),
        (shape(vectors.shape, F32), shape((vecs, vecs), F32)),
        [VMEM_SPEC] * 2,
        [pltpu.VMEM((vecs, vecs), F32)],
    )(gram, filtered)
    return basis, factor


def solution(mesh):
    chips = mesh.shape["rows"] // 2
    y = 8
    fine = Mesh(
        mesh.devices.reshape(chips // y, y, 2, mesh.shape["blk"]), ("z", "y", "core", "blk")
    )
    in_specs = (P("blk", ROWS), P(ROWS, None, "blk"), P(ROWS, "blk"), P(ROWS))
    out_specs = (P("blk", ROWS), P())
    return jax.shard_map(program, mesh=fine, in_specs=in_specs, out_specs=out_specs, check_vma=False)
```

```python
import functools

import jax
import jax.numpy as jnp
from jax import lax
from jax.experimental import pallas as pl
from jax.experimental.pallas import tpu as pltpu
from jax.sharding import Mesh, PartitionSpec as P

ROWS = ("z", "y", "core")
F32 = jnp.float32
BF16 = jnp.bfloat16
VMEM_SPEC = pl.BlockSpec(memory_space=pltpu.VMEM)
ANY_SPEC = pl.BlockSpec(memory_space=pl.ANY)
SMEM_SPEC = pl.BlockSpec(memory_space=pltpu.SMEM)


def call(kernel, out_shape, in_specs, scratch=(), mib=4):
    outs = jax.tree.map(lambda _: VMEM_SPEC, out_shape)
    return pl.pallas_call(
        kernel,
        out_shape=out_shape,
        in_specs=in_specs,
        out_specs=outs,
        scratch_shapes=scratch,
        compiler_params=pltpu.CompilerParams(vmem_limit_bytes=mib << 20),
    )


def shape(dims, dtype):
    return jax.ShapeDtypeStruct(dims, dtype)


def product_kernel(copies, index, *refs):
    pieces, (ham, out, tiles) = refs[:5], refs[5:]
    vecs = ham.shape[1]
    half = lax.broadcasted_iota(jnp.int16, (vecs, 128), 1) < jnp.int16(64)
    for p, piece in enumerate(pieces):
        for u in range(2):
            base = 32 * p + 16 * u
            start = here = piece[u, :, :128]
            for t in range(8):
                after = start if t == 7 else piece[u, :, 128 * (t + 1) : 128 * (t + 2)]
                tiles[base + 2 * t] = here
                tiles[base + 2 * t + 1] = pltpu.roll(jnp.where(half, after, here), 64, 1)
                here = after
    tiles[160] = jnp.zeros((vecs, 128), BF16)
    pairs = ham.shape[2] // 128

    def picked(row):
        return jnp.concatenate(
            [
                jnp.where(half, tiles[index[row, 2 * s]], tiles[index[row, 2 * s + 1]])
                for s in range(pairs)
            ],
            axis=1,
        )

    def two_rows(m, carry):
        sums = []
        for k in range(2):
            row = 2 * m + k
            sums.append(
                lax.dot_general(
                    picked(row), ham[row], (((1,), (1,)), ((), ())), preferred_element_type=F32
                )
            )
        both = jnp.concatenate(sums, axis=1).astype(BF16)
        lanes = pl.ds(pl.multiple_of(m * 128, 128), 128)
        for c in range(copies):
            out[c, :, lanes] = both
        return carry

    lax.fori_loop(0, ham.shape[0] // 2, two_rows, 0, unroll=4)


def index_kernel(total_blocks, block_rows, columns, counts, ham, out):
    core, blk = lax.axis_index("core"), lax.axis_index("blk")
    chip = lax.axis_index("z") * lax.axis_size("y") + lax.axis_index("y")
    slot = lax.broadcasted_iota(jnp.int32, columns.shape, 1)
    live = slot + blk * columns.shape[1] < counts[...]
    offset = (columns[...] - (chip - 2) * 2 * block_rows) & (total_blocks - 1)
    away, block = offset >> 5, offset & 15
    place = jnp.where(core == 0, away, 4 - away) * 32 + (offset & 16)
    tile = place + jnp.where((slot & 1) == 0, block, (block + 15) & 15)
    out[...] = jnp.where(live, tile, 160)


def first_kernel(parts, out):
    total = parts[0].astype(F32)
    for b in range(1, 4):
        total += parts[b].astype(F32)
    out[...] = total.astype(BF16)


def pair_kernel(mine, other, out):
    core = lax.axis_index("core")
    out[core] = mine[...]
    out[1 - core] = other[...]


LINES = (((7, 0, 64), (6, 0, 56), (0, 0, 8)), ((5, 0, 48), (4, 0, 40), (3, 0, 32), (1, 0, 8)))
REST = ((2, 0, 24), (1, 8, 8))
PACKED = 18 * 128


def turn(value, by):
    return pltpu.roll(value, by % 128, 1) if by % 128 else value


def pack(g):
    lane = lax.broadcasted_iota(jnp.int32, (8, 128), 1)
    row_lane = lax.broadcasted_iota(jnp.int32, (1, 128), 1)

    def side_by_side(group):
        at, line = 0, jnp.zeros((8, 128), F32)
        for strip, first, count in group:
            wide = jnp.concatenate(
                [g[8 * strip : 8 * strip + 8], jnp.zeros((8, 64), F32)], axis=1
            )
            line = jnp.where((lane >= at) & (lane < at + count), turn(wide, at - first), line)
            at += count
        return line

    rows = [line[r : r + 1] for line in map(side_by_side, LINES) for r in range(8)]
    rest = side_by_side(REST)
    for q in range(2):
        row = jnp.zeros((1, 128), F32)
        for p in range(4):
            here = (row_lane >= 32 * p) & (row_lane < 32 * p + 32)
            row = jnp.where(here, turn(rest[2 * p + q : 2 * p + q + 1], 32 * p), row)
        rows.append(row)
    return rows


def unpack(packed):
    lane = lax.broadcasted_iota(jnp.int32, (8, 128), 1)
    rows = [packed[:, 128 * r : 128 * r + 128] for r in range(18)]
    lines = [jnp.concatenate(rows[8 * q : 8 * q + 8], axis=0) for q in range(2)]
    rest = [turn(rows[16 + r % 2], -32 * (r // 2)) for r in range(8)]
    lines.append(jnp.concatenate(rest, axis=0))
    strips = [jnp.zeros((8, 128), F32) for _ in range(8)]
    for line, group in zip(lines, LINES + (REST,)):
        at = 0
        for strip, first, count in group:
            here = (lane >= first) & (lane < first + count)
            strips[strip] = jnp.where(here, turn(line, first - at), strips[strip])
            at += count
    low = jnp.concatenate([strip[:, :64] for strip in strips], axis=0)
    row = lax.broadcasted_iota(jnp.int32, (64, 64), 0) // 8
    col = lax.broadcasted_iota(jnp.int32, (64, 64), 1) // 8
    return jnp.where(col <= row, low, low.T)


def gram_kernel(parts, own, filtered, gram):
    total = parts[0].astype(F32)
    for b in range(1, 4):
        total += parts[b].astype(F32)
    value = (2.0 * total - own[lax.axis_index("core")].astype(F32)).astype(BF16)
    filtered[...] = value
    g = lax.dot_general(value, value, (((1,), (1,)), ((), ())), preferred_element_type=F32)
    for r, row in enumerate(pack(g)):
        for c in range(gram.shape[0]):
            gram[c, :, 128 * r : 128 * r + 128] = row


def sum_kernel(parts, out):
    total = parts[0]
    for c in range(1, parts.shape[0]):
        total += parts[c]
    for c in range(out.shape[0]):
        out[c] = total


def factor_kernel(scale, parts, filtered, basis, factor, scratch):
    total = parts[0]
    for c in range(1, 8):
        total += parts[c]
    whole = unpack(total * scale)
    lane = lax.broadcasted_iota(jnp.int32, (8, 128), 1)
    sub = lax.broadcasted_iota(jnp.int32, (8, 128), 0)
    zero = jnp.zeros((8, 64), F32)
    chunks = []
    for c in range(8):
        eye = jnp.where(lane - 64 == sub + 8 * c, F32(1.0), F32(0.0))
        wide = jnp.concatenate([whole[8 * c : 8 * c + 8], zero], axis=1)
        chunks.append(jnp.where(lane < 64, wide, eye))

    def spread(chunk, k):
        value = jnp.sum(jnp.where(lane == k, chunk, F32(0.0)), axis=1, keepdims=True)
        return jnp.broadcast_to(value, (8, 128))

    def down(value, r):
        return jnp.broadcast_to(value[r : r + 1], (8, 128))

    for b in range(8):
        cols = {c: [spread(chunks[c], 8 * b + j) for j in range(8)] for c in range(b, 8)}
        for r in range(8):
            row = down(chunks[b], r)
            heads = [down(cols[b][j], r) for j in range(r, 8)]
            inv = 1.0 / heads[0]
            for c in range(b if r < 7 else b + 1, 8):
                times = cols[c][r] * inv
                if c == b:
                    times = jnp.where(sub > r, times, F32(0.0))
                chunks[c] = chunks[c] - times * row
                for j in range(r + 1, 8):
                    cols[c][j] = cols[c][j] - times * heads[j - r]
    for c in range(8):
        pivot = jnp.where(lane == sub + 8 * c, chunks[c], F32(0.0))
        root = 1.0 / jnp.sqrt(jnp.sum(pivot, axis=1, keepdims=True))
        scaled = chunks[c] * root
        keep = jnp.where(lane >= sub + 8 * c, scaled, F32(0.0))
        factor[8 * c : 8 * c + 8, :] = keep[:, :64]
        scratch[8 * c : 8 * c + 8, :] = scaled[:, 64:]
    mine = scratch[pl.ds(pl.multiple_of(lax.axis_index("blk") * 16, 16), 16), :]
    total = jnp.zeros(basis.shape, F32)
    rest = mine
    parts = []
    for _ in range(3):
        top = rest.astype(BF16)
        parts.append(top)
        rest = rest - top.astype(F32)
    for top in reversed(parts):
        total += jnp.dot(top, filtered[...], preferred_element_type=F32)
    basis[...] = total


def from_chip(value, distance):
    chips = lax.axis_size("z") * lax.axis_size("y")
    pairs = []
    for c in range(chips):
        pairs.append((2 * ((c - distance) % chips), 2 * c))
        pairs.append((2 * ((c + distance) % chips) + 1, 2 * c + 1))
    return lax.ppermute(value, ROWS, pairs)


def flip(value):
    return lax.ppermute(value, "core", [(0, 1), (1, 0)])


def window(pair):
    near = from_chip(pair, 1)
    far = from_chip(pair, 2)
    near_other = flip(near)
    far_other = flip(far)
    return far, near, pair, near_other, far_other


def to_all(value, axes, count):
    return lax.all_to_all(
        jnp.broadcast_to(value[None], (count,) + value.shape), axes, 0, 0, tiled=True
    )


def program(vectors, hamiltonian, column_index, counts):
    block_rows = counts.shape[0]
    width = hamiltonian.shape[1]
    vecs = width
    total_blocks = block_rows * lax.axis_size(ROWS)
    index = call(
        functools.partial(index_kernel, total_blocks, block_rows),
        shape(column_index.shape, jnp.int32),
        [VMEM_SPEC] * 2 + [ANY_SPEC],
    )(column_index, counts.reshape(block_rows, 1), hamiltonian)

    def products(pieces, copies):
        return call(
            functools.partial(product_kernel, copies),
            shape((copies, vecs, block_rows * width), BF16),
            [SMEM_SPEC] + [VMEM_SPEC] * 6,
            [pltpu.VMEM((161, vecs, 128), BF16)],
            12,
        )(index, *pieces, hamiltonian)

    pair = to_all(vectors, ("core", "blk"), 8).reshape(2, vecs, block_rows * width)
    parts = products(window(pair), 4)
    parts = lax.all_to_all(parts, "blk", 0, 0, tiled=True)
    unit = shape((vecs, block_rows * width), BF16)
    first = call(first_kernel, unit, [VMEM_SPEC])(parts)
    pair_two = call(pair_kernel, shape(pair.shape, BF16), [VMEM_SPEC] * 2)(first, flip(first))
    parts = products(window(pair_two), 4)
    parts = lax.all_to_all(parts, "blk", 0, 0, tiled=True)
    filtered, gram = call(
        gram_kernel,
        (unit, shape((16, 1, PACKED), F32)),
        [VMEM_SPEC] * 2,
    )(parts, pair)
    gram = lax.all_to_all(gram, ("y", "core"), 0, 0, tiled=True)
    gram = call(sum_kernel, shape((8, 1, PACKED), F32), [VMEM_SPEC])(gram)
    gram = lax.all_to_all(gram, "z", 0, 0, tiled=True)
    basis, factor = call(
        functools.partial(factor_kernel, 1.0 / (total_blocks * width)),
        (shape(vectors.shape, F32), shape((vecs, vecs), F32)),
        [VMEM_SPEC] * 2,
        [pltpu.VMEM((vecs, vecs), F32)],
    )(gram, filtered)
    return basis, factor


def solution(mesh):
    chips = mesh.shape["rows"] // 2
    y = 8
    fine = Mesh(
        mesh.devices.reshape(chips // y, y, 2, mesh.shape["blk"]), ("z", "y", "core", "blk")
    )
    in_specs = (P("blk", ROWS), P(ROWS, None, "blk"), P(ROWS, "blk"), P(ROWS))
    out_specs = (P("blk", ROWS), P())
    return jax.shard_map(program, mesh=fine, in_specs=in_specs, out_specs=out_specs, check_vma=False)
```

```python
import functools

import jax
import jax.numpy as jnp
from jax import lax
from jax.experimental import pallas as pl
from jax.experimental.pallas import tpu as pltpu
from jax.sharding import Mesh, PartitionSpec as P

ROWS = ("z", "y", "core")
F32 = jnp.float32
BF16 = jnp.bfloat16
VMEM_SPEC = pl.BlockSpec(memory_space=pltpu.VMEM)
ANY_SPEC = pl.BlockSpec(memory_space=pl.ANY)
SMEM_SPEC = pl.BlockSpec(memory_space=pltpu.SMEM)


def call(kernel, out_shape, in_specs, scratch=(), mib=4):
    outs = jax.tree.map(lambda _: VMEM_SPEC, out_shape)
    return pl.pallas_call(
        kernel,
        out_shape=out_shape,
        in_specs=in_specs,
        out_specs=outs,
        scratch_shapes=scratch,
        compiler_params=pltpu.CompilerParams(vmem_limit_bytes=mib << 20),
    )


def shape(dims, dtype):
    return jax.ShapeDtypeStruct(dims, dtype)


PAIRS = tuple((slot, None) for slot in range(5))
UNITS = ((0, True), (0, False), (1, None), (2, None), (3, None), (4, True))


def product_kernel(copies, plan, index, *refs):
    pieces, (ham, out, tiles) = refs[: len(plan)], refs[len(plan) :]
    core = lax.axis_index("core")
    vecs = ham.shape[1]
    half = lax.broadcasted_iota(jnp.int16, (vecs, 128), 1) < jnp.int16(64)
    for piece, (slot, own) in zip(pieces, plan):
        if own is None:
            units = [(piece.at[u], 32 * slot + 16 * u) for u in range(2)]
        else:
            units = [(piece, 32 * slot + 16 * (core if own else 1 - core))]
        for unit, base in units:
            start = here = unit[:, :128]
            for t in range(8):
                after = start if t == 7 else unit[:, 128 * (t + 1) : 128 * (t + 2)]
                tiles[base + 2 * t] = here
                tiles[base + 2 * t + 1] = pltpu.roll(jnp.where(half, after, here), 64, 1)
                here = after
    tiles[160] = jnp.zeros((vecs, 128), BF16)
    pairs = ham.shape[2] // 128

    def picked(row):
        return jnp.concatenate(
            [
                jnp.where(half, tiles[index[row, 2 * s]], tiles[index[row, 2 * s + 1]])
                for s in range(pairs)
            ],
            axis=1,
        )

    def two_rows(m, carry):
        sums = []
        for k in range(2):
            row = 2 * m + k
            sums.append(
                lax.dot_general(
                    picked(row), ham[row], (((1,), (1,)), ((), ())), preferred_element_type=F32
                )
            )
        both = jnp.concatenate(sums, axis=1).astype(BF16)
        lanes = pl.ds(pl.multiple_of(m * 128, 128), 128)
        for c in range(copies):
            out[c, :, lanes] = both
        return carry

    lax.fori_loop(0, ham.shape[0] // 2, two_rows, 0, unroll=4)


def index_kernel(total_blocks, block_rows, columns, counts, ham, out):
    core, blk = lax.axis_index("core"), lax.axis_index("blk")
    chip = lax.axis_index("z") * lax.axis_size("y") + lax.axis_index("y")
    slot = lax.broadcasted_iota(jnp.int32, columns.shape, 1)
    live = slot + blk * columns.shape[1] < counts[...]
    offset = (columns[...] - (chip - 2) * 2 * block_rows) & (total_blocks - 1)
    away, block = offset >> 5, offset & 15
    place = jnp.where(core == 0, away, 4 - away) * 32 + (offset & 16)
    tile = place + jnp.where((slot & 1) == 0, block, (block + 15) & 15)
    out[...] = jnp.where(live, tile, 160)


def first_kernel(parts, out):
    total = parts[0].astype(F32)
    for b in range(1, 4):
        total += parts[b].astype(F32)
    out[...] = total.astype(BF16)


def pair_kernel(mine, other, out):
    core = lax.axis_index("core")
    out[core] = mine[...]
    out[1 - core] = other[...]


LINES = (((7, 0, 64), (6, 0, 56), (0, 0, 8)), ((5, 0, 48), (4, 0, 40), (3, 0, 32), (1, 0, 8)))
REST = ((2, 0, 24), (1, 8, 8))
PACKED = 18 * 128


def turn(value, by):
    return pltpu.roll(value, by % 128, 1) if by % 128 else value


def pack(g):
    lane = lax.broadcasted_iota(jnp.int32, (8, 128), 1)
    row_lane = lax.broadcasted_iota(jnp.int32, (1, 128), 1)

    def side_by_side(group):
        at, line = 0, jnp.zeros((8, 128), F32)
        for strip, first, count in group:
            wide = jnp.concatenate(
                [g[8 * strip : 8 * strip + 8], jnp.zeros((8, 64), F32)], axis=1
            )
            line = jnp.where((lane >= at) & (lane < at + count), turn(wide, at - first), line)
            at += count
        return line

    rows = [line[r : r + 1] for line in map(side_by_side, LINES) for r in range(8)]
    rest = side_by_side(REST)
    for q in range(2):
        row = jnp.zeros((1, 128), F32)
        for p in range(4):
            here = (row_lane >= 32 * p) & (row_lane < 32 * p + 32)
            row = jnp.where(here, turn(rest[2 * p + q : 2 * p + q + 1], 32 * p), row)
        rows.append(row)
    return rows


def unpack(packed):
    lane = lax.broadcasted_iota(jnp.int32, (8, 128), 1)
    rows = [packed[:, 128 * r : 128 * r + 128] for r in range(18)]
    lines = [jnp.concatenate(rows[8 * q : 8 * q + 8], axis=0) for q in range(2)]
    rest = [turn(rows[16 + r % 2], -32 * (r // 2)) for r in range(8)]
    lines.append(jnp.concatenate(rest, axis=0))
    strips = [jnp.zeros((8, 128), F32) for _ in range(8)]
    for line, group in zip(lines, LINES + (REST,)):
        at = 0
        for strip, first, count in group:
            here = (lane >= first) & (lane < first + count)
            strips[strip] = jnp.where(here, turn(line, first - at), strips[strip])
            at += count
    low = jnp.concatenate([strip[:, :64] for strip in strips], axis=0)
    row = lax.broadcasted_iota(jnp.int32, (64, 64), 0) // 8
    col = lax.broadcasted_iota(jnp.int32, (64, 64), 1) // 8
    return jnp.where(col <= row, low, low.T)


def gram_kernel(parts, own, filtered, gram):
    total = parts[0].astype(F32)
    for b in range(1, 4):
        total += parts[b].astype(F32)
    value = (2.0 * total - own[lax.axis_index("core")].astype(F32)).astype(BF16)
    filtered[...] = value
    g = lax.dot_general(value, value, (((1,), (1,)), ((), ())), preferred_element_type=F32)
    for r, row in enumerate(pack(g)):
        for c in range(gram.shape[0]):
            gram[c, :, 128 * r : 128 * r + 128] = row


def sum_kernel(parts, out):
    total = parts[0]
    for c in range(1, parts.shape[0]):
        total += parts[c]
    for c in range(out.shape[0]):
        out[c] = total


def factor_kernel(scale, parts, filtered, basis, factor, scratch):
    total = parts[0]
    for c in range(1, 8):
        total += parts[c]
    whole = unpack(total * scale)
    lane = lax.broadcasted_iota(jnp.int32, (8, 128), 1)
    sub = lax.broadcasted_iota(jnp.int32, (8, 128), 0)
    zero = jnp.zeros((8, 64), F32)
    chunks = []
    for c in range(8):
        eye = jnp.where(lane - 64 == sub + 8 * c, F32(1.0), F32(0.0))
        wide = jnp.concatenate([whole[8 * c : 8 * c + 8], zero], axis=1)
        chunks.append(jnp.where(lane < 64, wide, eye))

    def spread(chunk, k):
        value = jnp.sum(jnp.where(lane == k, chunk, F32(0.0)), axis=1, keepdims=True)
        return jnp.broadcast_to(value, (8, 128))

    def down(value, r):
        return jnp.broadcast_to(value[r : r + 1], (8, 128))

    for b in range(8):
        cols = {c: [spread(chunks[c], 8 * b + j) for j in range(8)] for c in range(b, 8)}
        for r in range(8):
            row = down(chunks[b], r)
            heads = [down(cols[b][j], r) for j in range(r, 8)]
            inv = 1.0 / heads[0]
            for c in range(b if r < 7 else b + 1, 8):
                times = cols[c][r] * inv
                if c == b:
                    times = jnp.where(sub > r, times, F32(0.0))
                chunks[c] = chunks[c] - times * row
                for j in range(r + 1, 8):
                    cols[c][j] = cols[c][j] - times * heads[j - r]
    for c in range(8):
        pivot = jnp.where(lane == sub + 8 * c, chunks[c], F32(0.0))
        root = 1.0 / jnp.sqrt(jnp.sum(pivot, axis=1, keepdims=True))
        scaled = chunks[c] * root
        keep = jnp.where(lane >= sub + 8 * c, scaled, F32(0.0))
        factor[8 * c : 8 * c + 8, :] = keep[:, :64]
        scratch[8 * c : 8 * c + 8, :] = scaled[:, 64:]
    mine = scratch[pl.ds(pl.multiple_of(lax.axis_index("blk") * 16, 16), 16), :]
    total = jnp.zeros(basis.shape, F32)
    rest = mine
    parts = []
    for _ in range(3):
        top = rest.astype(BF16)
        parts.append(top)
        rest = rest - top.astype(F32)
    for top in reversed(parts):
        total += jnp.dot(top, filtered[...], preferred_element_type=F32)
    basis[...] = total


def from_chip(value, distance):
    chips = lax.axis_size("z") * lax.axis_size("y")
    pairs = []
    for c in range(chips):
        pairs.append((2 * ((c - distance) % chips), 2 * c))
        pairs.append((2 * ((c + distance) % chips) + 1, 2 * c + 1))
    return lax.ppermute(value, ROWS, pairs)


def flip(value):
    return lax.ppermute(value, "core", [(0, 1), (1, 0)])


def window(pair):
    near = from_chip(pair, 1)
    far = from_chip(pair, 2)
    near_other = flip(near)
    far_other = flip(far)
    return far, near, pair, near_other, far_other


def unit_window(unit):
    ahead = from_chip(unit, -2)
    behind = from_chip(unit, 2)
    other = flip(unit)
    pair = call(pair_kernel, shape((2,) + unit.shape, BF16), [VMEM_SPEC] * 2)(unit, other)
    near = from_chip(pair, 1)
    crossed = flip(ahead)
    near_other = flip(near)
    return behind, crossed, near, pair, near_other, ahead


def to_all(value, axes, count):
    return lax.all_to_all(
        jnp.broadcast_to(value[None], (count,) + value.shape), axes, 0, 0, tiled=True
    )


def program(vectors, hamiltonian, column_index, counts):
    block_rows = counts.shape[0]
    width = hamiltonian.shape[1]
    vecs = width
    total_blocks = block_rows * lax.axis_size(ROWS)
    index = call(
        functools.partial(index_kernel, total_blocks, block_rows),
        shape(column_index.shape, jnp.int32),
        [VMEM_SPEC] * 2 + [ANY_SPEC],
    )(column_index, counts.reshape(block_rows, 1), hamiltonian)

    def products(pieces, plan, copies):
        return call(
            functools.partial(product_kernel, copies, plan),
            shape((copies, vecs, block_rows * width), BF16),
            [SMEM_SPEC] + [VMEM_SPEC] * (len(plan) + 1),
            [pltpu.VMEM((161, vecs, 128), BF16)],
            12,
        )(index, *pieces, hamiltonian)

    pair = to_all(vectors, ("core", "blk"), 8).reshape(2, vecs, block_rows * width)
    parts = products(window(pair), PAIRS, 4)
    parts = lax.all_to_all(parts, "blk", 0, 0, tiled=True)
    unit = shape((vecs, block_rows * width), BF16)
    first = call(first_kernel, unit, [VMEM_SPEC])(parts)
    parts = products(unit_window(first), UNITS, 4)
    parts = lax.all_to_all(parts, "blk", 0, 0, tiled=True)
    filtered, gram = call(
        gram_kernel,
        (unit, shape((16, 1, PACKED), F32)),
        [VMEM_SPEC] * 2,
    )(parts, pair)
    gram = lax.all_to_all(gram, ("y", "core"), 0, 0, tiled=True)
    gram = call(sum_kernel, shape((8, 1, PACKED), F32), [VMEM_SPEC])(gram)
    gram = lax.all_to_all(gram, "z", 0, 0, tiled=True)
    basis, factor = call(
        functools.partial(factor_kernel, 1.0 / (total_blocks * width)),
        (shape(vectors.shape, F32), shape((vecs, vecs), F32)),
        [VMEM_SPEC] * 2,
        [pltpu.VMEM((vecs, vecs), F32)],
    )(gram, filtered)
    return basis, factor


def solution(mesh):
    chips = mesh.shape["rows"] // 2
    y = 8
    fine = Mesh(
        mesh.devices.reshape(chips // y, y, 2, mesh.shape["blk"]), ("z", "y", "core", "blk")
    )
    in_specs = (P("blk", ROWS), P(ROWS, None, "blk"), P(ROWS, "blk"), P(ROWS))
    out_specs = (P("blk", ROWS), P())
    return jax.shard_map(program, mesh=fine, in_specs=in_specs, out_specs=out_specs, check_vma=False)
```
